32 devices in a mesh: dp: 4 (over y, x), seq: 4 (over z), head: 2 (over core).
Axes of the slice: x: 2, y: 2, z: 4, core: 2. Of those that a mesh axis runs over, the one named last changes fastest.
Arguments:
- latents: bfloat16 [4, 1024, 2048], P('dp', 'seq'), may hold values from -6 to 6
- w_qkv: bfloat16 [2048, 3, 1536], P(None, None, 'head'), may hold values from -0.125 to 0.125
- q_gain: float32 [128], replicated, may hold values from 0.1 to 1.9
- k_gain: float32 [128], replicated, may hold values from 0.1 to 1.9
- neighbours: int32 [16, 9], replicated, may hold values from -1 to 15, as said below
- grad_out: bfloat16 [4, 1024, 1536], P('dp', 'seq', 'head'), may hold values from -6 to 6
Outputs:
- attn_out: bfloat16 [4, 1024, 1536], P('dp', 'seq', 'head')
- grad_x: bfloat16 [4, 1024, 2048], P('dp', ('seq', 'head'))
- grad_w: float32 [2048, 3, 1536], P(('dp', 'seq'), None, 'head')
The draws below stay inside these ranges and needn't reach their ends.
Inputs may be any that keep to these rules, and one draw needn't show every extreme that they name: `neighbours`: row t lists only tiles whose slab differs from that of t (t // 4) by at most one and whose position in the slab (index % 4) differs by at most one, each at most once; t itself is always listed.
All inputs are finite; a program needn't handle non-finite values.
Results may differ from the reference program's by a relative error of at most 0.017.
Values may be sent and summed in bfloat16 or wider, within the bound.
A program may use at most 128 MiB of HBM per device.

```python
import math
import jax
import jax.numpy as jnp
from jax import lax

D = 2048
HEADS = 12
HD = 128
TILE = 64
GS = 4
SLAB = 256
TILES = 16
TOKENS = 1024
CLIPS = 4
HH = 1536


def draw_neighbours(key, part):
    tile_ids = jnp.arange(TILES, dtype=jnp.int32)
    slab_ids = tile_ids // GS
    column = tile_ids % GS
    reach = jax.random.randint(key, (TILES, 2), 0, 4)
    time_open = reach[:, 0] > 0
    space_open = reach[:, 1] > 0
    entries = []
    for time_step in (-1, 0, 1):
        for space_step in (-1, 0, 1):
            other_slab = slab_ids + time_step
            other_column = column + space_step
            inside = (other_slab >= 0) & (other_slab < TILES // GS) & (other_column >= 0) & (other_column < GS)
            open_time = jnp.logical_or(time_step == 0, time_open)
            open_space = jnp.logical_or(space_step == 0, space_open)
            keep = inside & open_time & open_space
            entries.append(jnp.where(keep, other_slab * GS + other_column, -1))
    return jnp.stack(entries, axis=1).astype(jnp.int32)


def with_spikes(values, own_key, source, target, shards_of, factor):
    def block_of(dim):
        return (jnp.arange(values.shape[dim]) // (values.shape[dim] // shards_of)).reshape((-1,) + (1,) * (values.ndim - 1 - dim))

    near = jax.random.permutation(own_key, shards_of)[block_of(target)]
    second = (block_of(target) + shards_of // 2) % shards_of
    return jnp.where((block_of(source) == near) | (block_of(source) == second), factor * values, values)


def block_scale(stream_key, dims, split, low, largest):
    level = 1.0
    for position, blocks in split:
        draws = jax.random.uniform(jax.random.fold_in(jax.random.fold_in(stream_key, 6), position), (blocks,), jnp.float32, low / len(split), largest / len(split))
        level = level * jnp.repeat(jnp.exp(draws), dims[position] // blocks).reshape((-1,) + (1,) * (len(dims) - 1 - position))
    return level


def normal_values(key, dims, deviation, most, shards=(), kind=jnp.bfloat16):
    array = jax.random.normal(key, dims, jnp.float32) * deviation
    if len(shards) > 0:
        array = block_scale(key, dims, shards, -0.22, 0.18) * array
    return jnp.clip(array, min=-most, max=most).astype(kind)


def gaussian_with(own_key, shape, deviation, most, pieces, heavy, held_as=jnp.bfloat16):
    array = deviation * jax.random.normal(own_key, shape, jnp.float32)
    if pieces:
        array = array * block_scale(own_key, shape, pieces, -0.22, 0.18)
    return jnp.clip(with_spikes(array, jax.random.fold_in(own_key, 3), *heavy), -most, most).astype(held_as)


def setup_inputs(seed: int = 0) -> dict:
    splits = jax.random.split(jax.random.key(seed), 7)
    return {
        "latents": gaussian_with(splits[0], (CLIPS, TOKENS, D), 1.0, 6.0, ((0, 4), (1, 4)), (1, 2, 4, 2.0)),
        "w_qkv": normal_values(splits[1], (D, 3, HH), D ** -0.5, 0.125, ((2, 2),)),
        "q_gain": jnp.clip(1.0 + 0.18 * jax.random.normal(splits[2], (HD,), jnp.float32), 0.1, 1.9),
        "k_gain": jnp.clip(1.0 + 0.18 * jax.random.normal(splits[3], (HD,), jnp.float32), 0.1, 1.9),
        "neighbours": draw_neighbours(jax.random.fold_in(splits[6], 71), 0),
        "grad_out": normal_values(splits[5], (CLIPS, TOKENS, HH), 1.0, 6.0, ((0, 4), (1, 4), (2, 2))),
    }


EPS = 1e-06

def inv_rms(values):
    return lax.rsqrt(lax.optimization_barrier(jnp.mean(values * values, axis=-1, keepdims=True)) + EPS)

def norm_back(raw, inverse, gain, upstream):
    normed = raw * inverse
    weighted = upstream * gain
    return inverse * (weighted - normed * lax.optimization_barrier(jnp.mean(weighted * normed, axis=-1, keepdims=True)))

def slab_allowed(neighbours, slab_index, tiles_slab):
    tile_total = neighbours.shape[0]
    first_query = (slab_index * tiles_slab).astype(jnp.int32)
    picked = lax.dynamic_slice_in_dim(neighbours, first_query, tiles_slab, 0)
    key_ids = (slab_index - 1) * tiles_slab + jnp.arange(3 * tiles_slab, dtype=jnp.int32)
    valid = (key_ids >= 0) & (key_ids < tile_total)
    hits = jnp.any(picked[:, :, None] == key_ids[None, None, :], axis=1) & valid[None, :]
    block = jnp.where(hits, 1.0, 0.0).astype(jnp.float32)
    return jnp.repeat(jnp.repeat(block, TILE, axis=0), TILE, axis=1)

def fold_rims(parts):
    lower = parts[:, :SLAB]
    middle = parts[:, SLAB:2 * SLAB]
    upper = parts[:, 2 * SLAB:]
    from_below = jnp.concatenate([jnp.zeros_like(upper[:1]), upper[:-1]], axis=0)
    from_above = jnp.concatenate([lower[1:], jnp.zeros_like(lower[:1])], axis=0)
    summed = middle + from_below + from_above
    return summed.reshape(summed.shape[0] * SLAB, HEADS, HD)

def clip_pass(latent_clip, cot_clip, w_flat, q_gain, k_gain, neighbours):
    token_count = latent_clip.shape[0]
    slab_count = token_count // SLAB
    score_scale = 1.0 / math.sqrt(HD)
    qkv = jnp.dot(latent_clip, w_flat, preferred_element_type=jnp.float32).reshape(token_count, 3, HEADS, HD)
    q_raw = qkv[:, 0]
    k_raw = qkv[:, 1]
    v_raw = qkv[:, 2]
    q_inv = inv_rms(q_raw)
    k_inv = inv_rms(k_raw)
    q_hat = lax.optimization_barrier((q_raw * q_inv * q_gain).astype(jnp.bfloat16))
    k_hat = lax.optimization_barrier((k_raw * k_inv * k_gain).astype(jnp.bfloat16))
    v_hat = lax.optimization_barrier(v_raw.astype(jnp.bfloat16))
    pad_keys = jnp.pad(k_hat, ((SLAB, SLAB), (0, 0), (0, 0)))
    pad_values = jnp.pad(v_hat, ((SLAB, SLAB), (0, 0), (0, 0)))

    def one_slab(slab_index):
        offset = (slab_index * SLAB).astype(jnp.int32)
        queries = lax.dynamic_slice_in_dim(q_hat, offset, SLAB, 0).astype(jnp.float32)
        keys = lax.dynamic_slice_in_dim(pad_keys, offset, 3 * SLAB, 0).astype(jnp.float32)
        values = lax.dynamic_slice_in_dim(pad_values, offset, 3 * SLAB, 0).astype(jnp.float32)
        upstream = lax.dynamic_slice_in_dim(cot_clip, offset, SLAB, 0).astype(jnp.float32)
        upstream = upstream.reshape(SLAB, HEADS, HD)
        allowed = slab_allowed(neighbours, slab_index, GS)
        scores = jnp.einsum('qhe,khe->hqk', queries, keys) * score_scale
        exponent = jnp.exp(scores) * allowed[None]
        row_total = lax.optimization_barrier(jnp.sum(exponent, axis=-1, keepdims=True))
        probs = exponent / row_total
        probs_b = lax.optimization_barrier(probs.astype(jnp.bfloat16)).astype(jnp.float32)
        attended = jnp.einsum('hqk,khe->qhe', probs_b, values)
        d_probs = jnp.einsum('qhe,khe->hqk', upstream, values)
        row_delta = lax.optimization_barrier(jnp.sum(probs * d_probs, axis=-1, keepdims=True))
        d_scores = (probs * (d_probs - row_delta) * score_scale).astype(jnp.bfloat16)
        d_scores = lax.optimization_barrier(d_scores).astype(jnp.float32)
        d_query = jnp.einsum('hqk,khe->qhe', d_scores, keys)
        d_keys = jnp.einsum('hqk,qhe->khe', d_scores, queries)
        d_values = jnp.einsum('hqk,qhe->khe', probs_b, upstream)
        return (attended.astype(jnp.bfloat16), d_query, d_keys, d_values)
    attended, d_qhat, d_kparts, d_vparts = lax.map(one_slab, jnp.arange(slab_count, dtype=jnp.int32))
    attended = attended.reshape(token_count, HEADS * HD)
    d_qhat = d_qhat.reshape(token_count, HEADS, HD)
    d_khat = fold_rims(d_kparts)
    d_value = fold_rims(d_vparts)
    d_query = norm_back(q_raw, q_inv, q_gain, d_qhat)
    d_key = norm_back(k_raw, k_inv, k_gain, d_khat)
    d_qkv = jnp.stack([d_query, d_key, d_value], axis=1).astype(jnp.bfloat16).reshape(token_count, 3 * HEADS * HD)
    grad_latent = jnp.dot(d_qkv, w_flat.T, preferred_element_type=jnp.float32).astype(jnp.bfloat16)
    weight_part = jnp.dot(latent_clip.T, d_qkv, preferred_element_type=jnp.float32)
    return (attended, grad_latent, weight_part)

def reference(latents, w_qkv, q_gain, k_gain, neighbours, grad_out):
    w_flat = w_qkv.reshape(D, 3 * HEADS * HD)

    def per_clip(pair):
        return clip_pass(pair[0], pair[1], w_flat, q_gain, k_gain, neighbours)
    attn_out, grad_x, weight_parts = lax.map(per_clip, (latents, grad_out))
    grad_w = lax.optimization_barrier(jnp.sum(weight_parts, axis=0)).reshape(D, 3, HEADS * HD)
    return (attn_out, grad_x, grad_w)
```

```python
import contextlib
import functools
import math

import jax
import jax.numpy as jnp
from jax import lax
from jax.experimental import pallas as pl
from jax.experimental.pallas import tpu as pltpu
from jax.sharding import PartitionSpec as P

MESH = pl.DeviceIdType.MESH

HD = 128
TILE = 64
PIECES = 2
AHEAD = 2


EPS = 1e-06


def scope(name):
    return contextlib.nullcontext()


def inv_rms(values):
    return lax.rsqrt(jnp.mean(values * values, axis=-1, keepdims=True) + EPS)


def norm_back(raw, inverse, gain, upstream):
    normed = raw * inverse
    weighted = upstream * gain
    return inverse * (weighted - normed * jnp.mean(weighted * normed, axis=-1, keepdims=True))


def nt(a, b):
    return lax.dot_general(a, b, (((1,), (1,)), ((), ())), preferred_element_type=jnp.float32)


def remote(src, dst, send_sem, recv_sem, peer):
    return pltpu.make_async_remote_copy(
        src_ref=src,
        dst_ref=dst,
        send_sem=send_sem,
        recv_sem=recv_sem,
        device_id=peer,
        device_id_type=MESH,
    )


def layer_kernel(
    n_dp, n_seq, n_head, lat_ref, w_ref, qg_ref, kg_ref, near_ref, do_ref,
    out_ref, gw_ref, gx_ref,
    gath, latt_ref, part, flow, gx_acc, gx_recv, gx_buf, lat_own, halo, w_buf, do_buf,
    q_raw, k_raw, q_hat, k_hat, v_hat, mask, mask_t, stat, stat_t, clip_buf, out_buf, gw_buf,
    qg_buf, kg_buf, near_buf,
    l_sem, w_sem, a_ss, a_rs, f_ss, f_rs, o_ss, o_rs, s_ss, s_rs, c_ss, c_rs,
    d_ss, d_rs, z_ss, z_rs, h_ss, h_rs, out_sem, gw_sem, gx_sem,
):
    three, model_width, head_width = w_ref.shape
    slab = lat_ref.shape[0]
    items = gath.shape[0]
    chunks, _, rows, width = part.shape
    group = width // HD
    parts = chunks // three
    heads = head_width // HD
    pieces, _, piece, _ = halo.shape
    sub = piece // n_head
    block = model_width // n_dp
    scale = 1.0 / math.sqrt(HD)
    me_dp = lax.axis_index("dp")
    me_seq = lax.axis_index("seq")
    me_head = lax.axis_index("head")
    below = me_seq > 0
    above = me_seq < n_seq - 1

    def dp_peer(step, sign=1):
        if n_dp == 4:
            low, high = lax.rem(me_dp, 2), me_dp // 2
            if step % 2:
                low = 1 - low
            if step // 2:
                high = 1 - high
            return high * 2 + low
        return lax.rem(me_dp + n_dp + sign * step, n_dp)

    def head_peer(step, sign=1):
        return lax.rem(me_head + n_head + sign * step, n_head)

    def cols(p):
        return pl.ds(pl.multiple_of(p * width, width), width)

    def at(h):
        return pl.ds(pl.multiple_of(h * HD, HD), HD)

    barrier = pltpu.get_barrier_semaphore()

    @pl.when(below)
    def _():
        pl.semaphore_signal(barrier, inc=1, device_id={"seq": me_seq - 1}, device_id_type=MESH)

    @pl.when(above)
    def _():
        pl.semaphore_signal(barrier, inc=1, device_id={"seq": me_seq + 1}, device_id_type=MESH)

    for step in range(1, n_dp):
        pl.semaphore_signal(
            barrier, inc=1, device_id={"dp": dp_peer(step, -1)}, device_id_type=MESH
        )
    for step in range(1, n_head):
        pl.semaphore_signal(
            barrier, inc=1, device_id={"head": head_peer(step, -1)}, device_id_type=MESH
        )

    own_lat = pltpu.make_async_copy(lat_ref, lat_own, l_sem.at[0])
    own_do = pltpu.make_async_copy(do_ref, do_buf.at[1], l_sem.at[1])
    small = [
        pltpu.make_async_copy(near_ref, near_buf, l_sem.at[2]),
        pltpu.make_async_copy(qg_ref, qg_buf, l_sem.at[3]),
        pltpu.make_async_copy(kg_ref, kg_buf, l_sem.at[4]),
    ]

    def w_copy(kind, p):
        return pltpu.make_async_copy(
            w_ref.at[kind, :, cols(p)], w_buf.at[kind, :, cols(p)], w_sem.at[kind * parts + p]
        )

    for copy in small:
        copy.start()
    own_lat.start()
    for kind in range(three):
        @pl.loop(0, parts)
        def _(p):
            w_copy(kind, p).start()
    own_do.start()

    for copy in small:
        copy.wait()
    tiles = near_ref.shape[0]
    near = near_buf[...]
    tile_ids = lax.broadcasted_iota(jnp.int32, (tiles, tiles), 1)
    hits = jnp.zeros((tiles, tiles), jnp.float32)
    for slot in range(near_ref.shape[1]):
        hits = jnp.where(near[:, slot : slot + 1] == tile_ids, 1.0, hits)
    hits = hits.astype(jnp.bfloat16)
    own_tile = me_seq * (slab // TILE)
    first_tile = own_tile - slab // TILE
    own_pick = lax.broadcasted_iota(jnp.int32, (slab, tiles), 1) == (
        lax.broadcasted_iota(jnp.int32, (slab, tiles), 0) // TILE + own_tile
    )
    own_pick = jnp.where(own_pick, 1.0, 0.0).astype(jnp.bfloat16)
    wide_pick = lax.broadcasted_iota(jnp.int32, (tiles, 3 * slab), 0) == (
        lax.broadcasted_iota(jnp.int32, (tiles, 3 * slab), 1) // TILE + first_tile
    )
    wide_pick = jnp.where(wide_pick, 1.0, 0.0).astype(jnp.bfloat16)
    picked = jnp.dot(own_pick, hits, preferred_element_type=jnp.float32).astype(jnp.bfloat16)
    mask[...] = jnp.dot(picked, wide_pick, preferred_element_type=jnp.float32)
    picked = lax.dot_general(
        own_pick, hits, (((1,), (1,)), ((), ())), preferred_element_type=jnp.float32
    ).astype(jnp.bfloat16)
    mask_t[...] = jnp.dot(picked, wide_pick, preferred_element_type=jnp.float32)

    def clear(side):
        for j in range(pieces):
            halo[j, side] = jnp.zeros_like(halo[j, side])
        do_buf[2 * side] = jnp.zeros_like(do_buf[2 * side])
        stat_t[2 * side] = jnp.ones_like(stat_t[2 * side])

    @pl.when(me_seq == 0)
    def _():
        clear(0)

    @pl.when(me_seq == n_seq - 1)
    def _():
        clear(1)

    q_gain = qg_buf[...]
    k_gain = kg_buf[...]

    sides = jnp.minimum(me_seq, 1) + jnp.minimum(n_seq - 1 - me_seq, 1)
    with scope("BARRIER"):
        pl.semaphore_wait(barrier, n_dp - 1 + n_head - 1 + sides)

    sub_rows = pl.ds(pl.multiple_of(me_head * sub, sub), sub)

    def lat_copy(side, j):
        return remote(
            lat_ref.at[pl.ds(pl.multiple_of(j * piece + me_head * sub, sub), sub)],
            halo.at[j, 1 - side, sub_rows],
            a_ss.at[side, j], a_rs.at[side, j], {"seq": me_seq + 2 * side - 1},
        )

    def do_copy(side):
        return remote(
            do_ref, do_buf.at[2 - 2 * side],
            o_ss.at[side], o_rs.at[side], {"seq": me_seq + 2 * side - 1},
        )

    def stat_copy(side):
        return remote(
            stat_t.at[1], stat_t.at[2 - 2 * side],
            s_ss.at[side], s_rs.at[side], {"seq": me_seq + 2 * side - 1},
        )

    def pass_copy(side, j, step):
        return remote(
            halo.at[j, side, sub_rows], halo.at[j, side, sub_rows],
            f_ss.at[side, j, step - 1], f_rs.at[side, j, step - 1],
            {"head": head_peer(step)},
        )

    def clip_copy(step):
        peer = dp_peer(step)
        return remote(
            lat_ref.at[:, pl.ds(pl.multiple_of(peer * block, block), block)],
            clip_buf.at[step - 1], c_ss.at[step - 1], c_rs.at[step - 1], {"dp": peer},
        )

    for j in range(pieces):
        @pl.when(below)
        def _():
            lat_copy(0, j).start()

        @pl.when(above)
        def _():
            lat_copy(1, j).start()

    for step in range(1, n_dp):
        clip_copy(step).start()

    @pl.when(below)
    def _():
        do_copy(0).start()

    @pl.when(above)
    def _():
        do_copy(1).start()

    def normed(raw, gain):
        found = []
        for h in range(group):
            head = raw[:, h * HD : (h + 1) * HD]
            found.append((head * inv_rms(head) * gain).astype(jnp.bfloat16))
        return jnp.concatenate(found, axis=1)

    own_lat.wait()

    for kind in range(three):
        with scope("OWN%d" % kind):
            @pl.loop(0, parts)
            def _(p):
                w_copy(kind, p).wait()
                raw = jnp.dot(
                    lat_own[...], w_buf[kind, :, cols(p)], preferred_element_type=jnp.float32
                )
                if kind == 0:
                    q_raw[:, cols(p)] = raw
                    q_hat[1, :, cols(p)] = normed(raw, q_gain)
                elif kind == 1:
                    k_raw[:, cols(p)] = raw
                    k_hat[1, :, cols(p)] = normed(raw, k_gain)
                else:
                    v_hat[1, :, cols(p)] = raw.astype(jnp.bfloat16)

    def arrive(j):
        @pl.when(above)
        def _():
            lat_copy(0, j).wait_recv()
            for step in range(1, n_head):
                pass_copy(1, j, step).start()

        @pl.when(below)
        def _():
            lat_copy(1, j).wait_recv()
            for step in range(1, n_head):
                pass_copy(0, j, step).start()

        @pl.when(above)
        def _():
            for step in range(1, n_head):
                pass_copy(1, j, step).wait_recv()

        @pl.when(below)
        def _():
            for step in range(1, n_head):
                pass_copy(0, j, step).wait_recv()

    def halo_part(kind, j, p):
        raw = jnp.dot(
            halo[j].reshape(2 * piece, model_width), w_buf[kind, :, cols(p)],
            preferred_element_type=jnp.float32,
        )
        if kind == 2:
            kept, value = v_hat, raw.astype(jnp.bfloat16)
        else:
            kept, value = ((q_hat, k_hat)[kind], normed(raw, (q_gain, k_gain)[kind]))
        at_rows = slice(j * piece, (j + 1) * piece)
        kept[0, at_rows, cols(p)] = value[:piece]
        kept[2, at_rows, cols(p)] = value[piece:]

    for j in range(pieces - 1):
        with scope("ARRIVE%d" % j):
            arrive(j)
        for kind in (1, 2, 0):
            with scope("HALO%d" % kind):
                @pl.loop(0, parts)
                def _(p):
                    halo_part(kind, j, p)

    with scope("ARRIVEL"):
        arrive(pieces - 1)

    def put(item, value):
        gath[item, 0] = value.astype(jnp.bfloat16)

    def place(position):
        late = jnp.maximum(position - parts, 0)
        is_late = jnp.where(position >= parts, 1, 0)
        kind = is_late * (1 + lax.rem(late, 2))
        p = is_late * (late // 2) + (1 - is_late) * position
        return kind, cols(p)

    relay = n_dp == 4
    direct = (1, 2) if relay else tuple(range(1, n_dp))
    half = slab // 2
    first, second = slice(0, half), slice(half, slab)

    def dp_copy(i, step):
        return remote(
            gath.at[i, 0], gath.at[i, step],
            d_ss.at[i, step - 1], d_rs.at[i, step - 1], {"dp": dp_peer(step)},
        )

    def relay_copy(i, via):
        which = (first, second)[via - 1]
        return remote(
            gath.at[i, via, which], gath.at[i, 3, which],
            d_ss.at[i, 1 + via], d_rs.at[i, 1 + via], {"dp": dp_peer(3 - via)},
        )

    def send_own(i):
        for step in direct:
            dp_copy(i, step).start()

    def pass_on(i):
        for step in direct:
            dp_copy(i, step).wait_recv()
            if relay:
                relay_copy(i, step).start()

    def hop(side, c, t):
        peer = lax.rem(me_seq + n_seq + 1 - 2 * side, n_seq)
        return remote(
            flow.at[side, c, t], flow.at[side, c, t],
            z_ss.at[side, c, t], z_rs.at[side, c, t], {"seq": peer},
        )

    fed = (below, above)

    def onward(side, t):
        return t < me_seq if side else t > me_seq

    def stage(side, c):
        @pl.loop(0, n_seq)
        def _(turn):
            t = turn if side else n_seq - 1 - turn

            @pl.when(onward(side, t))
            def _():
                @pl.when(fed[side])
                def _():
                    hop(side, c, t).wait_recv()
                    summed = part[c, t] + flow[side, c, t].astype(jnp.float32)
                    flow[side, c, t] = summed.astype(jnp.bfloat16)

                @pl.when(jnp.logical_not(fed[side]))
                def _():
                    flow[side, c, t] = part[c, t].astype(jnp.bfloat16)

                hop(side, c, t).start()

    def paired(ref, c):
        found = [ref(c * group + j) for j in range(group)]
        return jnp.concatenate(found, axis=1)

    def input_share(c):
        kind, where = place(c)
        gx_acc[...] += nt(paired(lambda i: gath[i, 0], c), w_buf[kind, :, where])

    def weight_share(c):
        if relay:
            for j in range(group):
                for via in (1, 2):
                    relay_copy(c * group + j, via).wait_recv()
        everyone = paired(lambda i: gath[i].reshape(n_dp * slab, HD), c)
        product = jnp.dot(latt_ref[...], everyone, preferred_element_type=jnp.float32)
        part[c] = product.reshape(n_seq, rows, width)

    own_do.wait()
    lanes = lax.broadcasted_iota(jnp.int32, (slab, 128), 1)
    stat[...] = jnp.zeros_like(stat)

    def out_copy(p):
        return pltpu.make_async_copy(
            out_buf.at[:, cols(p)], out_ref.at[:, cols(p)], out_sem.at[p]
        )

    def forward(h):
        queries = q_hat[1, :, at(h)]
        keys = k_hat[:, :, at(h)].reshape(3 * slab, HD)
        values = v_hat[:, :, at(h)].reshape(3 * slab, HD)
        expo = jnp.exp(nt(queries, keys) * scale) * mask[...]
        row_total = jnp.sum(expo, axis=-1, keepdims=True)
        probs = expo * (1.0 / row_total)
        out_buf[:, at(h)] = jnp.dot(
            probs.astype(jnp.bfloat16), values, preferred_element_type=jnp.float32
        ).astype(jnp.bfloat16)
        d_probs = nt(do_buf[1, :, at(h)], values)
        row_delta = jnp.sum(probs * d_probs, axis=-1, keepdims=True)
        d_scores = (probs * (d_probs - row_delta) * scale).astype(jnp.bfloat16)
        d_qhat = jnp.dot(d_scores, keys, preferred_element_type=jnp.float32)
        raw = q_raw[:, at(h)]
        put(h, norm_back(raw, inv_rms(raw), q_gain, d_qhat))
        kept = jnp.where(lanes == 2 * h, row_total, stat[...])
        stat[...] = jnp.where(lanes == 2 * h + 1, row_delta, kept)

    early = max(heads - AHEAD * group, 0)

    @pl.loop(0, parts)
    def _(p):
        with scope("HALOKV"):
            halo_part(1, pieces - 1, p)
            halo_part(2, pieces - 1, p)

        @pl.loop(0, group)
        def _(j):
            h = p * group + j
            with scope("FWD"):
                forward(h)
                send_own(h)

            @pl.when(h >= heads - early)
            def _():
                with scope("PASSE"):
                    pass_on(h - (heads - early))

        out_copy(p).start()

    stat_t[1] = jnp.transpose(stat[...])[: stat_t.shape[1]]

    @pl.when(below)
    def _():
        stat_copy(0).start()

    @pl.when(above)
    def _():
        stat_copy(1).start()

    own_cols = pl.ds(pl.multiple_of(me_dp * block, block), block)
    with scope("CLIP"):
        latt_ref[:, :slab] = jnp.transpose(lat_own[:, own_cols])
        for step in range(1, n_dp):
            clip_copy(step).wait_recv()
            latt_ref[:, step * slab : (step + 1) * slab] = jnp.transpose(clip_buf[step - 1])

    gx_acc[...] = jnp.zeros_like(gx_acc)

    def reverse(h):
        keys = k_hat[1, :, at(h)]
        values = v_hat[1, :, at(h)]
        queries = q_hat[:, :, at(h)].reshape(3 * slab, HD)
        upstream = do_buf[:, :, at(h)].reshape(3 * slab, HD)
        total = jnp.concatenate([stat_t[s, pl.ds(2 * h, 1), :] for s in range(3)], axis=1)
        delta = jnp.concatenate([stat_t[s, pl.ds(2 * h + 1, 1), :] for s in range(3)], axis=1)
        probs = jnp.exp(nt(keys, queries) * scale) * mask_t[...] * (1.0 / total)
        late = (parts + 2 * (h // group)) * group + lax.rem(h, group)
        put(late + group, jnp.dot(probs.astype(jnp.bfloat16), upstream, preferred_element_type=jnp.float32))
        d_scores = (probs * (nt(values, upstream) - delta) * scale).astype(jnp.bfloat16)
        d_khat = jnp.dot(d_scores, queries, preferred_element_type=jnp.float32)
        raw = k_raw[:, at(h)]
        put(late, norm_back(raw, inv_rms(raw), k_gain, d_khat))

    share = gx_ref.shape[0]

    def h_copy(step):
        peer = head_peer(step)
        return remote(
            gx_acc.at[pl.ds(pl.multiple_of(peer * share, share), share)],
            gx_recv.at[step - 1], h_ss.at[step - 1], h_rs.at[step - 1], {"head": peer},
        )

    gx_out = pltpu.make_async_copy(gx_buf, gx_ref, gx_sem.at[0])

    def gw_copy(c):
        kind, where = place(c)
        return pltpu.make_async_copy(gw_buf.at[c], gw_ref.at[kind, :, where], gw_sem.at[c])

    def finish(c):
        gw_buf[c] = part[c, me_seq]
        for side in range(2):
            @pl.when(fed[side])
            def _():
                hop(side, c, me_seq).wait_recv()
                gw_buf[c] += flow[side, c, me_seq].astype(jnp.float32)
        gw_copy(c).start()

    @pl.loop(0, chunks + n_seq)
    def _(tick):
        @pl.when(tick < chunks)
        def _():
            with scope("WSHARE"):
                weight_share(tick)

        for side in range(2):
            lag = n_seq - 1 - me_seq if side else me_seq
            c = tick - lag

            @pl.when((c >= 0) & (c < chunks))
            def _():
                with scope("STAGE%d" % side):
                    stage(side, c)

        @pl.when(tick == 0)
        def _():
            with scope("HALOQ"):
                @pl.loop(0, parts)
                def _(p):
                    halo_part(0, pieces - 1, p)

            @pl.when(above)
            def _():
                with scope("DOW"):
                    do_copy(0).wait_recv()
                    stat_copy(0).wait_recv()

            @pl.when(below)
            def _():
                with scope("DOW"):
                    do_copy(1).wait_recv()
                    stat_copy(1).wait_recv()

        @pl.when(tick < parts)
        def _():
            with scope("REV"):
                @pl.loop(0, group)
                def _(j):
                    reverse(tick * group + j)

        for j in range(group):
            @pl.when(tick < chunks - early // group)
            def _():
                with scope("PASSON"):
                    pass_on(tick * group + j + early)

            @pl.when(tick < chunks - parts)
            def _():
                send_own(tick * group + j + heads)

        @pl.when(tick < chunks)
        def _():
            with scope("INSHARE"):
                input_share(tick)

        @pl.when(tick == chunks - 1)
        def _():
            for step in range(1, n_head):
                h_copy(step).start()

        @pl.when(tick == chunks)
        def _():
            with scope("GX"):
                for step in range(1, n_head):
                    h_copy(step).wait()
                total = gx_acc[pl.ds(pl.multiple_of(me_head * share, share), share)]
                for step in range(1, n_head):
                    total = total + gx_recv[step - 1]
                gx_buf[...] = total.astype(gx_buf.dtype)
                gx_out.start()

        @pl.when(tick >= n_seq)
        def _():
            with scope("FINAL"):
                finish(tick - n_seq)

    with scope("SETTLE"):
        @pl.loop(0, chunks)
        def _(c):
            gw_copy(c).wait()
            for side in range(2):
                @pl.loop(0, n_seq)
                def _(t):
                    @pl.when(onward(side, t))
                    def _():
                        hop(side, c, t).wait_send()

        @pl.loop(0, items)
        def _(i):
            for step in direct:
                dp_copy(i, step).wait_send()
                if relay:
                    relay_copy(i, step).wait_send()

        @pl.loop(0, parts)
        def _(p):
            out_copy(p).wait()

        gx_out.wait()

        def settle(side):
            do_copy(side).wait_send()
            stat_copy(side).wait_send()
            for j in range(pieces):
                lat_copy(side, j).wait_send()
                for step in range(1, n_head):
                    pass_copy(side, j, step).wait_send()

        @pl.when(below)
        def _():
            settle(0)

        @pl.when(above)
        def _():
            settle(1)

        for step in range(1, n_dp):
            clip_copy(step).wait_send()


def layer(slab_tokens, w_three, q_gain, k_gain, neighbours, upstream):
    n_dp, n_seq, n_head = (lax.axis_size(axis) for axis in ("dp", "seq", "head"))
    slab = slab_tokens.shape[0]
    three, model_width, head_width = w_three.shape
    heads = head_width // HD
    group = 2 if heads % 2 == 0 else 1
    width = group * HD
    chunks = three * heads // group
    items = three * heads
    block = model_width // n_dp
    rows = block // n_seq
    share = slab // n_head
    pieces = PIECES
    piece = slab // pieces
    stat_rows = -(-2 * heads // 8) * 8
    relays = 4 if n_dp == 4 else n_dp - 1
    anywhere = pl.BlockSpec(memory_space=pl.ANY)
    in_hbm = pl.BlockSpec(memory_space=pltpu.MemorySpace.HBM)
    dma = pltpu.SemaphoreType.DMA
    bf16, f32 = jnp.bfloat16, jnp.float32
    return pl.pallas_call(
        functools.partial(layer_kernel, n_dp, n_seq, n_head),
        out_shape=(
            jax.ShapeDtypeStruct((slab, head_width), bf16),
            jax.ShapeDtypeStruct((three, rows, head_width), f32),
            jax.ShapeDtypeStruct((share, model_width), bf16),
        ),
        in_specs=[in_hbm] * 6,
        out_specs=(anywhere,) * 3,
        scratch_shapes=[
            pltpu.VMEM((items, n_dp, slab, HD), bf16),
            pltpu.VMEM((block, n_dp * slab), bf16),
            pltpu.VMEM((chunks, n_seq, rows, width), f32),
            pltpu.VMEM((2, chunks, n_seq, rows, width), bf16),
            pltpu.VMEM((slab, model_width), f32),
            pltpu.VMEM((n_head - 1, share, model_width), f32),
            pltpu.VMEM((share, model_width), bf16),
            pltpu.VMEM((slab, model_width), bf16),
            pltpu.VMEM((pieces, 2, piece, model_width), bf16),
            pltpu.VMEM((three, model_width, head_width), bf16),
            pltpu.VMEM((3, slab, head_width), bf16),
            pltpu.VMEM((slab, head_width), f32),
            pltpu.VMEM((slab, head_width), f32),
            pltpu.VMEM((3, slab, head_width), bf16),
            pltpu.VMEM((3, slab, head_width), bf16),
            pltpu.VMEM((3, slab, head_width), bf16),
            pltpu.VMEM((slab, 3 * slab), f32),
            pltpu.VMEM((slab, 3 * slab), f32),
            pltpu.VMEM((slab, 128), f32),
            pltpu.VMEM((3, stat_rows, slab), f32),
            pltpu.VMEM((n_dp - 1, slab, block), bf16),
            pltpu.VMEM((slab, head_width), bf16),
            pltpu.VMEM((chunks, rows, width), f32),
            pltpu.VMEM((1, HD), f32),
            pltpu.VMEM((1, HD), f32),
            pltpu.VMEM(neighbours.shape, jnp.int32),
            dma((5,)),
            dma((chunks,)),
            dma((2, pieces)),
            dma((2, pieces)),
            dma((2, pieces, n_head - 1)),
            dma((2, pieces, n_head - 1)),
            dma((2,)),
            dma((2,)),
            dma((2,)),
            dma((2,)),
            dma((n_dp - 1,)),
            dma((n_dp - 1,)),
            dma((items, relays)),
            dma((items, relays)),
            dma((2, chunks, n_seq)),
            dma((2, chunks, n_seq)),
            dma((n_head - 1,)),
            dma((n_head - 1,)),
            dma((chunks // three,)),
            dma((chunks,)),
            dma((1,)),
        ],
        compiler_params=pltpu.CompilerParams(
            collective_id=0, has_side_effects=True, vmem_limit_bytes=52 * 1024 * 1024
        ),
        name="layer",
    )(slab_tokens, w_three, q_gain.reshape(1, HD), k_gain.reshape(1, HD), neighbours, upstream)


def local(latents, w_qkv, q_gain, k_gain, neighbours, grad_out):
    w_three = jnp.transpose(w_qkv, (1, 0, 2))
    attn_out, grad_w, grad_x = layer(
        latents[0], w_three, q_gain, k_gain, neighbours, grad_out[0]
    )
    return (attn_out[None], grad_x[None], jnp.transpose(grad_w, (1, 0, 2)))


def solution(mesh):
    in_specs = (P("dp", "seq", None), P(None, None, "head"), P(), P(), P(), P("dp", "seq", "head"))
    out_specs = (
        P("dp", "seq", "head"),
        P("dp", ("seq", "head"), None),
        P(("dp", "seq"), None, "head"),
    )
    return jax.shard_map(local, mesh=mesh, in_specs=in_specs, out_specs=out_specs, check_vma=False)
```

```python
import contextlib
import functools
import math

import jax
import jax.numpy as jnp
from jax import lax
from jax.experimental import pallas as pl
from jax.experimental.pallas import tpu as pltpu
from jax.sharding import PartitionSpec as P

MESH = pl.DeviceIdType.MESH

HD = 128
TILE = 64
PIECES = 2
PASS_LAG = 2
PRODUCT_LAG = 4
HOP_LAG = 2
NEAR_LAST = 8
STATS = 4


EPS = 1e-06


def scope(name):
    return contextlib.nullcontext()


def inv_rms(values):
    return lax.rsqrt(jnp.mean(values * values, axis=-1, keepdims=True) + EPS)


def norm_back(raw, inverse, gain, upstream):
    normed = raw * inverse
    weighted = upstream * gain
    return inverse * (weighted - normed * jnp.mean(weighted * normed, axis=-1, keepdims=True))


def nt(a, b):
    return lax.dot_general(a, b, (((1,), (1,)), ((), ())), preferred_element_type=jnp.float32)


def remote(src, dst, send_sem, recv_sem, peer):
    return pltpu.make_async_remote_copy(
        src_ref=src,
        dst_ref=dst,
        send_sem=send_sem,
        recv_sem=recv_sem,
        device_id=peer,
        device_id_type=MESH,
    )


def drain(ref, sem):
    pltpu.make_async_copy(ref, ref, sem).wait()


def layer_kernel(
    n_dp, n_seq, n_head, lat_ref, w_ref, qg_ref, kg_ref, near_ref, do_ref,
    out_ref, gw_ref, gx_ref,
    gath, latt_ref, part, flow, gx_acc, gx_recv, gx_buf, lat_own, halo, w_buf, do_buf,
    q_raw, k_raw, q_hat, k_hat, v_hat, mask, mask_t, stat, stat_t, clip_buf, out_buf, gw_buf,
    qg_buf, kg_buf, near_buf,
    l_sem, w_sem, a_ss, a_rs, f_ss, f_rs, o_ss, o_rs, s_ss, s_rs, c_ss, c_rs,
    d_ss, d_rs, z_ss, z_rs, h_ss, h_rs, out_sem, gw_sem, gx_sem,
):
    three, model_width, head_width = w_ref.shape
    slab = lat_ref.shape[0]
    items, _, rows, _ = part.shape
    heads = head_width // HD
    group = 2 if heads % 2 == 0 else 1
    width = group * HD
    parts = heads // group
    chunks = three * parts
    pieces, _, piece, _ = halo.shape
    sub = piece // n_head
    block = model_width // n_dp
    scale = 1.0 / math.sqrt(HD)
    me_dp = lax.axis_index("dp")
    me_seq = lax.axis_index("seq")
    me_head = lax.axis_index("head")
    below = me_seq > 0
    above = me_seq < n_seq - 1

    def dp_peer(step, sign=1):
        if n_dp == 4:
            low, high = lax.rem(me_dp, 2), me_dp // 2
            if step % 2:
                low = 1 - low
            if step // 2:
                high = 1 - high
            return high * 2 + low
        return lax.rem(me_dp + n_dp + sign * step, n_dp)

    def head_peer(step, sign=1):
        return lax.rem(me_head + n_head + sign * step, n_head)

    def cols(p):
        return pl.ds(pl.multiple_of(p * width, width), width)

    def at(h):
        return pl.ds(pl.multiple_of(h * HD, HD), HD)

    barrier = pltpu.get_barrier_semaphore()

    @pl.when(below)
    def _():
        pl.semaphore_signal(barrier, inc=1, device_id={"seq": me_seq - 1}, device_id_type=MESH)

    @pl.when(above)
    def _():
        pl.semaphore_signal(barrier, inc=1, device_id={"seq": me_seq + 1}, device_id_type=MESH)

    for step in range(1, n_dp):
        pl.semaphore_signal(
            barrier, inc=1, device_id={"dp": dp_peer(step, -1)}, device_id_type=MESH
        )
    for step in range(1, n_head):
        pl.semaphore_signal(
            barrier, inc=1, device_id={"head": head_peer(step, -1)}, device_id_type=MESH
        )

    own_lat = pltpu.make_async_copy(lat_ref, lat_own, l_sem.at[0])
    own_do = pltpu.make_async_copy(do_ref, do_buf.at[1], l_sem.at[1])
    small = [
        pltpu.make_async_copy(near_ref, near_buf, l_sem.at[2]),
        pltpu.make_async_copy(qg_ref, qg_buf, l_sem.at[3]),
        pltpu.make_async_copy(kg_ref, kg_buf, l_sem.at[4]),
    ]

    def w_copy(kind):
        return pltpu.make_async_copy(w_ref.at[kind], w_buf.at[kind], w_sem.at[kind])

    for copy in small:
        copy.start()
    own_lat.start()
    for kind in range(three):
        w_copy(kind).start()
    own_do.start()

    for copy in small:
        copy.wait()
    tiles = near_ref.shape[0]
    near = near_buf[...]
    tile_ids = lax.broadcasted_iota(jnp.int32, (tiles, tiles), 1)
    hits = jnp.zeros((tiles, tiles), jnp.float32)
    for slot in range(near_ref.shape[1]):
        hits = jnp.where(near[:, slot : slot + 1] == tile_ids, 1.0, hits)
    hits = hits.astype(jnp.bfloat16)
    own_tile = me_seq * (slab // TILE)
    first_tile = own_tile - slab // TILE
    own_pick = lax.broadcasted_iota(jnp.int32, (slab, tiles), 1) == (
        lax.broadcasted_iota(jnp.int32, (slab, tiles), 0) // TILE + own_tile
    )
    own_pick = jnp.where(own_pick, 1.0, 0.0).astype(jnp.bfloat16)
    wide_pick = lax.broadcasted_iota(jnp.int32, (tiles, 3 * slab), 0) == (
        lax.broadcasted_iota(jnp.int32, (tiles, 3 * slab), 1) // TILE + first_tile
    )
    wide_pick = jnp.where(wide_pick, 1.0, 0.0).astype(jnp.bfloat16)
    picked = jnp.dot(own_pick, hits, preferred_element_type=jnp.float32).astype(jnp.bfloat16)
    mask[...] = jnp.dot(picked, wide_pick, preferred_element_type=jnp.float32)
    picked = lax.dot_general(
        own_pick, hits, (((1,), (1,)), ((), ())), preferred_element_type=jnp.float32
    ).astype(jnp.bfloat16)
    mask_t[...] = jnp.dot(picked, wide_pick, preferred_element_type=jnp.float32)

    def clear(side):
        for j in range(pieces):
            halo[j, side] = jnp.zeros_like(halo[j, side])
        do_buf[2 * side] = jnp.zeros_like(do_buf[2 * side])
        stat_t[2 * side] = jnp.ones_like(stat_t[2 * side])

    @pl.when(me_seq == 0)
    def _():
        clear(0)

    @pl.when(me_seq == n_seq - 1)
    def _():
        clear(1)

    q_gain = qg_buf[...]
    k_gain = kg_buf[...]

    sides = jnp.minimum(me_seq, 1) + jnp.minimum(n_seq - 1 - me_seq, 1)
    with scope("BARRIER"):
        pl.semaphore_wait(barrier, n_dp - 1 + n_head - 1 + sides)

    sub_rows = pl.ds(pl.multiple_of(me_head * sub, sub), sub)

    def lat_copy(side, j):
        return remote(
            lat_ref.at[pl.ds(pl.multiple_of(j * piece + me_head * sub, sub), sub)],
            halo.at[j, 1 - side, sub_rows],
            a_ss.at[side], a_rs.at[side, j], {"seq": me_seq + 2 * side - 1},
        )

    def do_copy(side):
        return remote(
            do_ref, do_buf.at[2 - 2 * side],
            o_ss.at[side], o_rs.at[side], {"seq": me_seq + 2 * side - 1},
        )

    def stat_rows(m):
        return pl.ds(pl.multiple_of(m * 2 * STATS, 2 * STATS), 2 * STATS)

    def stat_copy(side, m):
        return remote(
            stat_t.at[1, stat_rows(m)], stat_t.at[2 - 2 * side, stat_rows(m)],
            s_ss.at[side], s_rs.at[side, m], {"seq": me_seq + 2 * side - 1},
        )

    def pass_copy(side, j, step):
        return remote(
            halo.at[j, side, sub_rows], halo.at[j, side, sub_rows],
            f_ss.at[side, step - 1], f_rs.at[side, j, step - 1],
            {"head": head_peer(step)},
        )

    def clip_copy(step):
        peer = dp_peer(step)
        return remote(
            lat_ref.at[:, pl.ds(pl.multiple_of(peer * block, block), block)],
            clip_buf.at[step - 1], c_ss.at[0], c_rs.at[step - 1], {"dp": peer},
        )

    for j in range(pieces):
        @pl.when(below)
        def _():
            lat_copy(0, j).start()

        @pl.when(above)
        def _():
            lat_copy(1, j).start()

    for step in range(1, n_dp):
        clip_copy(step).start()

    @pl.when(below)
    def _():
        do_copy(0).start()

    @pl.when(above)
    def _():
        do_copy(1).start()

    def normed(raw, gain):
        found = []
        for h in range(group):
            head = raw[:, h * HD : (h + 1) * HD]
            found.append((head * inv_rms(head) * gain).astype(jnp.bfloat16))
        return jnp.concatenate(found, axis=1)

    own_lat.wait()

    for kind in range(three):
        with scope("OWN%d" % kind):
            w_copy(kind).wait()

            @pl.loop(0, parts)
            def _(p):
                raw = jnp.dot(
                    lat_own[...], w_buf[kind, :, cols(p)], preferred_element_type=jnp.float32
                )
                if kind == 0:
                    q_raw[:, cols(p)] = raw
                    q_hat[1, :, cols(p)] = normed(raw, q_gain)
                elif kind == 1:
                    k_raw[:, cols(p)] = raw
                    k_hat[1, :, cols(p)] = normed(raw, k_gain)
                else:
                    v_hat[1, :, cols(p)] = raw.astype(jnp.bfloat16)

    def arrive(j):
        @pl.when(above)
        def _():
            lat_copy(0, j).wait_recv()
            for step in range(1, n_head):
                pass_copy(1, j, step).start()

        @pl.when(below)
        def _():
            lat_copy(1, j).wait_recv()
            for step in range(1, n_head):
                pass_copy(0, j, step).start()

        @pl.when(above)
        def _():
            for step in range(1, n_head):
                pass_copy(1, j, step).wait_recv()

        @pl.when(below)
        def _():
            for step in range(1, n_head):
                pass_copy(0, j, step).wait_recv()

    def halo_part(kind, j, p):
        raw = jnp.dot(
            halo[j].reshape(2 * piece, model_width), w_buf[kind, :, cols(p)],
            preferred_element_type=jnp.float32,
        )
        if kind == 2:
            kept, value = v_hat, raw.astype(jnp.bfloat16)
        else:
            kept, value = ((q_hat, k_hat)[kind], normed(raw, (q_gain, k_gain)[kind]))
        at_rows = slice(j * piece, (j + 1) * piece)
        kept[0, at_rows, cols(p)] = value[:piece]
        kept[2, at_rows, cols(p)] = value[piece:]

    for j in range(pieces - 1):
        with scope("ARRIVE%d" % j):
            arrive(j)
        for kind in (1, 2, 0):
            with scope("HALO%d" % kind):
                @pl.loop(0, parts)
                def _(p):
                    halo_part(kind, j, p)

    own_cols = pl.ds(pl.multiple_of(me_dp * block, block), block)
    with scope("CLIP"):
        latt_ref[:, :slab] = jnp.transpose(lat_own[:, own_cols])
        for step in range(1, n_dp):
            clip_copy(step).wait_recv()
            latt_ref[:, step * slab : (step + 1) * slab] = jnp.transpose(clip_buf[step - 1])

    gx_acc[...] = jnp.zeros_like(gx_acc)

    with scope("ARRIVEL"):
        arrive(pieces - 1)

    def put(item, value):
        gath[item, 0] = value.astype(jnp.bfloat16)

    def place(i):
        late = jnp.maximum(i - heads, 0)
        is_late = jnp.where(i >= heads, 1, 0)
        kind = is_late * (1 + lax.rem(late, 2))
        return kind, is_late * (late // 2) + (1 - is_late) * i

    relay = n_dp == 4
    direct = (1, 2) if relay else tuple(range(1, n_dp))
    half = slab // 2
    first, second = slice(0, half), slice(half, slab)

    def dp_copy(i, step):
        return remote(
            gath.at[i, 0], gath.at[i, step],
            d_ss.at[step - 1], d_rs.at[i, step - 1], {"dp": dp_peer(step)},
        )

    def relay_copy(i, via):
        which = (first, second)[via - 1]
        return remote(
            gath.at[i, via, which], gath.at[i, 3, which],
            d_ss.at[1 + via], d_rs.at[i, 1 + via], {"dp": dp_peer(3 - via)},
        )

    def send_own(i):
        for step in direct:
            dp_copy(i, step).start()

    def pass_on(i):
        for step in direct:
            dp_copy(i, step).wait_recv()
            if relay:
                relay_copy(i, step).start()

    def hop(side, c, t):
        peer = lax.rem(me_seq + n_seq + 1 - 2 * side, n_seq)
        return remote(
            flow.at[side, c, t], flow.at[side, c, t],
            z_ss.at[side, t], z_rs.at[side, c, t], {"seq": peer},
        )

    fed = (below, above)

    def onward(side, t):
        return t < me_seq if side else t > me_seq

    def hand_on(side, c, t):
        @pl.when(onward(side, t))
        def _():
            @pl.when(fed[side])
            def _():
                hop(side, c, t).wait_recv()
                summed = part[c, t] + flow[side, c, t].astype(jnp.float32)
                flow[side, c, t] = summed.astype(jnp.bfloat16)

            @pl.when(jnp.logical_not(fed[side]))
            def _():
                flow[side, c, t] = part[c, t].astype(jnp.bfloat16)

            hop(side, c, t).start()

    def near(side):
        return me_seq - 1 if side else me_seq + 1

    def stage(side, c):
        @pl.loop(0, n_seq)
        def _(turn):
            t = turn if side else n_seq - 1 - turn

            @pl.when((t != near(side)) | fed[side] | (c < items - NEAR_LAST))
            def _():
                hand_on(side, c, t)

        @pl.when((c == items - 1) & jnp.logical_not(fed[side]))
        def _():
            @pl.loop(max(items - NEAR_LAST, 0), items)
            def _(late):
                hand_on(side, late, near(side))

    def input_share(c):
        late = jnp.maximum(c - parts, 0)
        is_late = jnp.where(c >= parts, 1, 0)
        kind = is_late * (1 + lax.rem(late, 2))
        p = is_late * (late // 2) + (1 - is_late) * c
        found = []
        for j in range(group):
            h = p * group + j
            found.append(gath[is_late * (heads + h + kind - 1) + h, 0])
        gx_acc[...] += nt(jnp.concatenate(found, axis=1), w_buf[kind, :, cols(p)])

    def weight_share(i):
        if relay:
            for via in (1, 2):
                relay_copy(i, via).wait_recv()
        product = jnp.dot(
            latt_ref[...], gath[i].reshape(n_dp * slab, HD), preferred_element_type=jnp.float32
        )
        part[i] = product.reshape(n_seq, rows, HD)

    own_do.wait()
    lanes = lax.broadcasted_iota(jnp.int32, (slab, 128), 1)
    stat[...] = jnp.zeros_like(stat)

    def out_copy(p):
        return pltpu.make_async_copy(
            out_buf.at[:, cols(p)], out_ref.at[:, cols(p)], out_sem.at[0]
        )

    def forward(h):
        queries = q_hat[1, :, at(h)]
        keys = k_hat[:, :, at(h)].reshape(3 * slab, HD)
        values = v_hat[:, :, at(h)].reshape(3 * slab, HD)
        expo = jnp.exp(nt(queries, keys) * scale) * mask[...]
        row_total = jnp.sum(expo, axis=-1, keepdims=True)
        probs = expo * (1.0 / row_total)
        out_buf[:, at(h)] = jnp.dot(
            probs.astype(jnp.bfloat16), values, preferred_element_type=jnp.float32
        ).astype(jnp.bfloat16)
        d_probs = nt(do_buf[1, :, at(h)], values)
        row_delta = jnp.sum(probs * d_probs, axis=-1, keepdims=True)
        d_scores = (probs * (d_probs - row_delta) * scale).astype(jnp.bfloat16)
        d_qhat = jnp.dot(d_scores, keys, preferred_element_type=jnp.float32)
        raw = q_raw[:, at(h)]
        put(h, norm_back(raw, inv_rms(raw), q_gain, d_qhat))
        kept = jnp.where(lanes == 2 * h, row_total, stat[...])
        stat[...] = jnp.where(lanes == 2 * h + 1, row_delta, kept)

    gx_acc[...] = jnp.zeros_like(gx_acc)

    def reverse(h):
        keys = k_hat[1, :, at(h)]
        values = v_hat[1, :, at(h)]
        queries = q_hat[:, :, at(h)].reshape(3 * slab, HD)
        upstream = do_buf[:, :, at(h)].reshape(3 * slab, HD)
        total = jnp.concatenate([stat_t[s, pl.ds(2 * h, 1), :] for s in range(3)], axis=1)
        delta = jnp.concatenate([stat_t[s, pl.ds(2 * h + 1, 1), :] for s in range(3)], axis=1)
        probs = jnp.exp(nt(keys, queries) * scale) * mask_t[...] * (1.0 / total)
        late = heads + 2 * h
        put(late + 1, jnp.dot(probs.astype(jnp.bfloat16), upstream, preferred_element_type=jnp.float32))
        d_scores = (probs * (nt(values, upstream) - delta) * scale).astype(jnp.bfloat16)
        d_khat = jnp.dot(d_scores, queries, preferred_element_type=jnp.float32)
        raw = k_raw[:, at(h)]
        put(late, norm_back(raw, inv_rms(raw), k_gain, d_khat))

    share = gx_ref.shape[0]

    def h_copy(step):
        peer = head_peer(step)
        return remote(
            gx_acc.at[pl.ds(pl.multiple_of(peer * share, share), share)],
            gx_recv.at[step - 1], h_ss.at[step - 1], h_rs.at[step - 1], {"head": peer},
        )

    gx_out = pltpu.make_async_copy(gx_buf, gx_ref, gx_sem.at[0])

    def gw_copy(i):
        kind, h = place(i)
        return pltpu.make_async_copy(gw_buf.at[i], gw_ref.at[kind, :, at(h)], gw_sem.at[0])

    def finish(c):
        gw_buf[c] = part[c, me_seq]
        for side in range(2):
            @pl.when(fed[side])
            def _():
                hop(side, c, me_seq).wait_recv()
                gw_buf[c] += flow[side, c, me_seq].astype(jnp.float32)
        gw_copy(c).start()

    def settle_items():
        for step in direct:
            drain(gath.at[:, 0], d_ss.at[step - 1])
            if relay:
                drain(gath.at[:, 0, first], d_ss.at[1 + step])
        drain(out_buf, out_sem.at[0])
        drain(clip_buf, c_ss.at[0])

        def settle(side):
            do_copy(side).wait_send()
            drain(stat_t.at[1], s_ss.at[side])
            drain(halo.at[:, side, pl.ds(0, sub)], a_ss.at[side])
            for step in range(1, n_head):
                drain(halo.at[:, side, pl.ds(0, sub)], f_ss.at[side, step - 1])

        @pl.when(below)
        def _():
            settle(0)

        @pl.when(above)
        def _():
            settle(1)

    def settle_hops():
        for side in range(2):
            @pl.loop(0, n_seq)
            def _(t):
                @pl.when(onward(side, t))
                def _():
                    drain(flow.at[side, :, t], z_ss.at[side, t])

    product_end = items + PRODUCT_LAG
    gx_tick = heads + 2 * heads - 1 + 2 * parts
    ticks = max(product_end + HOP_LAG * max(n_seq - 2, 0), gx_tick + 1)
    finish_lag = product_end + HOP_LAG * (n_seq - 1) + 1 - items
    in_loop = max(min(items - NEAR_LAST, ticks - finish_lag), 0)

    def product(tick):
        with scope("WSHARE"):
            weight_share(tick - PRODUCT_LAG)

    def stages(tick):
        for side in range(2):
            lag = n_seq - 1 - me_seq if side else me_seq
            c = tick - PRODUCT_LAG - HOP_LAG * lag

            @pl.when((c >= 0) & (c < items))
            def _():
                with scope("STAGE%d" % side):
                    stage(side, c)

    def pass_next(tick):
        with scope("PASSON"):
            pass_on(tick - PASS_LAG)

    def query_part(p):
        with scope("HALOQ"):
            halo_part(0, pieces - 1, p)

    @pl.loop(0, heads)
    def _(tick):
        @pl.when(lax.rem(tick, group) == 0)
        def _():
            with scope("HALOKV"):
                halo_part(1, pieces - 1, tick // group)
                halo_part(2, pieces - 1, tick // group)

        with scope("FWD"):
            forward(tick)

        @pl.when((lax.rem(tick, STATS) == STATS - 1) | (tick == heads - 1))
        def _():
            m = tick // STATS
            turned = jnp.transpose(stat[...])
            for k in range(stat_t.shape[1] // (2 * STATS)):
                @pl.when(m == k)
                def _():
                    at_rows = slice(k * 2 * STATS, (k + 1) * 2 * STATS)
                    stat_t[1, at_rows] = turned[at_rows]

            @pl.when(below)
            def _():
                stat_copy(0, m).start()

            @pl.when(above)
            def _():
                stat_copy(1, m).start()

        @pl.when(tick == heads - 1)
        def _():
            query_part(0)

        @pl.when(tick >= PRODUCT_LAG)
        def _():
            product(tick)
            stages(tick)

        @pl.when(tick >= PASS_LAG)
        def _():
            pass_next(tick)

        send_own(tick)

        @pl.when(lax.rem(tick, group) == group - 1)
        def _():
            out_copy(tick // group).start()

    @pl.loop(heads, ticks)
    def _(tick):
        turn = tick - heads
        odd = lax.rem(turn, 2) == 1
        reversing = (turn == 0) | odd & (turn < 2 * heads - 1)

        @pl.when(tick < items + PASS_LAG)
        def _():
            pass_next(tick)

        for side, has in ((0, above), (1, below)):
            @pl.when((turn == 0) & has)
            def _():
                with scope("DOW"):
                    do_copy(side).wait_recv()

            @pl.when(reversing & has & (lax.rem((turn + 1) // 2, STATS) == 0))
            def _():
                with scope("STW"):
                    stat_copy(side, (turn + 1) // 2 // STATS).wait_recv()

        @pl.when(reversing)
        def _():
            with scope("REV"):
                reverse((turn + 1) // 2)

        @pl.when(turn == 0)
        def _():
            send_own(heads)

        @pl.when(tick + 1 < items)
        def _():
            send_own(tick + 1)

        @pl.when((lax.rem(turn, 2 * group) == 2 * group - 2) & (turn < 2 * heads - 2 * group))
        def _():
            query_part((turn + 2) // (2 * group))

        @pl.when((turn >= 2) & jnp.logical_not(odd) & (turn // 2 - 1 < chunks - parts))
        def _():
            with scope("INSHARE"):
                input_share(turn // 2 - 1)

        @pl.when(odd & (turn >= 2 * heads - 1) & (turn < 2 * heads - 1 + 2 * parts))
        def _():
            with scope("INSHARE"):
                input_share(chunks - 1 - (turn - 2 * heads + 1) // 2)

        @pl.when(tick < product_end)
        def _():
            product(tick)

        stages(tick)

        @pl.when(tick == gx_tick)
        def _():
            for step in range(1, n_head):
                h_copy(step).start()

        c = tick - finish_lag

        @pl.when((c >= 0) & (c < in_loop))
        def _():
            with scope("FINAL"):
                finish(c)

        @pl.when(tick == product_end)
        def _():
            with scope("SETTLEI"):
                settle_items()

    with scope("GX"):
        for step in range(1, n_head):
            h_copy(step).wait()
        total = gx_acc[pl.ds(pl.multiple_of(me_head * share, share), share)]
        for step in range(1, n_head):
            total = total + gx_recv[step - 1]
        gx_buf[...] = total.astype(gx_buf.dtype)
        gx_out.start()

    @pl.loop(in_loop, items)
    def _(c):
        with scope("FINAL"):
            finish(c)

    with scope("SETTLE"):
        settle_hops()
        drain(gw_buf, gw_sem.at[0])
        gx_out.wait()


def layer(slab_tokens, w_three, q_gain, k_gain, neighbours, upstream):
    n_dp, n_seq, n_head = (lax.axis_size(axis) for axis in ("dp", "seq", "head"))
    slab = slab_tokens.shape[0]
    three, model_width, head_width = w_three.shape
    heads = head_width // HD
    items = three * heads
    block = model_width // n_dp
    rows = block // n_seq
    share = slab // n_head
    pieces = PIECES
    piece = slab // pieces
    stat_rows = -(-2 * heads // 8) * 8
    relays = 4 if n_dp == 4 else n_dp - 1
    anywhere = pl.BlockSpec(memory_space=pl.ANY)
    in_hbm = pl.BlockSpec(memory_space=pltpu.MemorySpace.HBM)
    dma = pltpu.SemaphoreType.DMA
    bf16, f32 = jnp.bfloat16, jnp.float32
    return pl.pallas_call(
        functools.partial(layer_kernel, n_dp, n_seq, n_head),
        out_shape=(
            jax.ShapeDtypeStruct((slab, head_width), bf16),
            jax.ShapeDtypeStruct((three, rows, head_width), f32),
            jax.ShapeDtypeStruct((share, model_width), bf16),
        ),
        in_specs=[in_hbm] * 6,
        out_specs=(anywhere,) * 3,
        scratch_shapes=[
            pltpu.VMEM((items, n_dp, slab, HD), bf16),
            pltpu.VMEM((block, n_dp * slab), bf16),
            pltpu.VMEM((items, n_seq, rows, HD), f32),
            pltpu.VMEM((2, items, n_seq, rows, HD), bf16),
            pltpu.VMEM((slab, model_width), f32),
            pltpu.VMEM((n_head - 1, share, model_width), f32),
            pltpu.VMEM((share, model_width), bf16),
            pltpu.VMEM((slab, model_width), bf16),
            pltpu.VMEM((pieces, 2, piece, model_width), bf16),
            pltpu.VMEM((three, model_width, head_width), bf16),
            pltpu.VMEM((3, slab, head_width), bf16),
            pltpu.VMEM((slab, head_width), f32),
            pltpu.VMEM((slab, head_width), f32),
            pltpu.VMEM((3, slab, head_width), bf16),
            pltpu.VMEM((3, slab, head_width), bf16),
            pltpu.VMEM((3, slab, head_width), bf16),
            pltpu.VMEM((slab, 3 * slab), f32),
            pltpu.VMEM((slab, 3 * slab), f32),
            pltpu.VMEM((slab, 128), f32),
            pltpu.VMEM((3, stat_rows, slab), f32),
            pltpu.VMEM((n_dp - 1, slab, block), bf16),
            pltpu.VMEM((slab, head_width), bf16),
            pltpu.VMEM((items, rows, HD), f32),
            pltpu.VMEM((1, HD), f32),
            pltpu.VMEM((1, HD), f32),
            pltpu.VMEM(neighbours.shape, jnp.int32),
            dma((5,)),
            dma((three,)),
            dma((2,)),
            dma((2, pieces)),
            dma((2, n_head - 1)),
            dma((2, pieces, n_head - 1)),
            dma((2,)),
            dma((2,)),
            dma((2,)),
            dma((2, stat_rows // (2 * STATS))),
            dma((1,)),
            dma((n_dp - 1,)),
            dma((relays,)),
            dma((items, relays)),
            dma((2, n_seq)),
            dma((2, items, n_seq)),
            dma((n_head - 1,)),
            dma((n_head - 1,)),
            dma((1,)),
            dma((1,)),
            dma((1,)),
        ],
        compiler_params=pltpu.CompilerParams(
            collective_id=0, has_side_effects=True, vmem_limit_bytes=48 * 1024 * 1024
        ),
        name="layer",
    )(slab_tokens, w_three, q_gain, k_gain, neighbours, upstream)


def deliver_kernel(*refs):
    count = len(refs) // 3
    sources, targets, sems = refs[:count], refs[count : 2 * count], refs[2 * count :]
    copies = [pltpu.make_async_copy(*three) for three in zip(sources, targets, sems)]
    for copy in copies:
        copy.start()
    for copy in copies:
        copy.wait()


def deliver(*arrays):
    anywhere = pl.BlockSpec(memory_space=pl.ANY)
    return pl.pallas_call(
        deliver_kernel,
        out_shape=tuple(jax.ShapeDtypeStruct(x.shape, x.dtype) for x in arrays),
        in_specs=[anywhere] * len(arrays),
        out_specs=(anywhere,) * len(arrays),
        scratch_shapes=[pltpu.SemaphoreType.DMA] * len(arrays),
        compiler_params=pltpu.CompilerParams(vmem_limit_bytes=1024 * 1024),
        name="deliver",
    )(*arrays)


def local(latents, w_qkv, q_gain, k_gain, neighbours, grad_out):
    w_three = jnp.transpose(w_qkv, (1, 0, 2))
    latents, w_three, q_gain, k_gain, neighbours, grad_out = (
        pltpu.with_memory_space_constraint(x, pltpu.MemorySpace.HBM)
        for x in (
            latents[0], w_three, q_gain.reshape(1, HD), k_gain.reshape(1, HD), neighbours, grad_out[0]
        )
    )
    found = layer(latents, w_three, q_gain, k_gain, neighbours, grad_out)
    attn_out, grad_w, grad_x = deliver(*found)
    return (attn_out[None], grad_x[None], jnp.transpose(grad_w, (1, 0, 2)))


def solution(mesh):
    in_specs = (P("dp", "seq", None), P(None, None, "head"), P(), P(), P(), P("dp", "seq", "head"))
    out_specs = (
        P("dp", "seq", "head"),
        P("dp", ("seq", "head"), None),
        P(("dp", "seq"), None, "head"),
    )
    return jax.shard_map(local, mesh=mesh, in_specs=in_specs, out_specs=out_specs, check_vma=False)
```
